32 devices in a mesh: pb: 8 (over z, x), ka: 4 (over y, core).
Axes of the slice: x: 2, y: 2, z: 4, core: 2. Of those that a mesh axis runs over, the one named last changes fastest.
Arguments:
- node_states: float32 [512, 256], P('pb'), may hold values from -17 to 17
- frames: float32 [12, 512], P(None, 'pb'), may hold values from -20 to 20, as said below
- edge_states: bfloat16 [512, 512, 128], P('pb', 'ka'), may hold values from -6 to 6
- chain_number: int32 [512], replicated, may hold values from 0 to 3, as said below
- residue_index: int32 [512], replicated, may hold values from 0 to 767, as said below
- padding_mask: int32 [512], replicated, may hold values from 0 to 1, as said below
- query_weight: bfloat16 [256, 2048], replicated, may hold values from -0.375 to 0.375
- key_weight: bfloat16 [256, 2048], replicated, may hold values from -0.375 to 0.375
- value_weight: bfloat16 [256, 2048], replicated, may hold values from -0.375 to 0.375
- point_query: bfloat16 [256, 192], replicated, may hold values from -0.375 to 0.375
- point_key: bfloat16 [256, 192], replicated, may hold values from -0.375 to 0.375
- point_value: bfloat16 [256, 288], replicated, may hold values from -0.375 to 0.375
- bias_weight: bfloat16 [128, 8], replicated, may hold values from -0.5 to 0.5
- point_gamma: float32 [8], replicated, may hold values from 0.3 to 3
- relpos_table: float32 [128, 128], replicated, may hold values from -3 to 3
- output_weight: bfloat16 [3456, 256], replicated, may hold values from -0.109375 to 0.109375
- attention_scales: float32 [256], replicated, may hold values from 0.5 to 1.5
- layer_project: bfloat16 [2, 256, 768], replicated, may hold values from -0.375 to 0.375
- layer_output: bfloat16 [2, 256, 256], replicated, may hold values from -0.375 to 0.375
- layer_expand: bfloat16 [2, 256, 256], replicated, may hold values from -0.375 to 0.375
- layer_shrink: bfloat16 [2, 256, 256], replicated, may hold values from -0.375 to 0.375
- layer_scales: float32 [2, 2, 256], replicated, may hold values from 0.5 to 1.5
- frame_weight: float32 [256, 6], replicated, may hold values from -0.375 to 0.375
- node_to_edge: bfloat16 [256, 768], replicated, may hold values from -0.375 to 0.375
- edge_first: bfloat16 [128, 384], replicated, may hold values from -0.5 to 0.5
- edge_second: bfloat16 [384, 384], replicated, may hold values from -0.3125 to 0.3125
- edge_third: bfloat16 [384, 128], replicated, may hold values from -0.3125 to 0.3125
- edge_biases: float32 [2, 384], replicated, may hold values from -3 to 3
- edge_scales: float32 [128], replicated, may hold values from 0.5 to 1.5
Outputs:
- node_out: float32 [512, 256], P('pb')
- frames_out: float32 [12, 512], P(None, 'pb')
- edges_out: bfloat16 [512, 512, 128], P('pb', 'ka')
The draws below stay inside these ranges and needn't reach their ends.
Inputs may be any that keep to these rules, and one draw needn't show every extreme that they name: `chain_number`: never falls from one residue to the next; the first residue has 0 and the last 3. `residue_index`: rises by 1 or 2 from one residue to the next, starting at 0; exactly 256 of the rises are 2. `padding_mask`: the ones come first; at least 256 residues are ones and at least one is padding. `frames`: rows 0 to 8 form a proper rotation of each residue.
All inputs are finite; a program needn't handle non-finite values.
Results may differ from the reference program's by a relative error of at most 0.025.
Values may be sent and summed in bfloat16 or wider, within the bound.
A program may use at most 128 MiB of HBM per device.

```python
import math
import jax
import jax.numpy as jnp
from jax import lax

C_S = 256
C_Z = 128
HEADS = 8
HD = 256
QKP = 8
VP = 12
EH = 384
RELBINS = 128
LAYERS = 2
N = 512
QD = 64
TF_HD = 64
N_PB = 8


def draw_structure(key):
    position = jnp.arange(N, dtype=jnp.int32)
    bounds = jax.random.randint(jax.random.fold_in(key, 101), (3,), 1, N)
    chains = jnp.sum((position[:, None] >= bounds[None, :]).astype(jnp.int32), axis=1).astype(jnp.int32)
    order = jax.random.permutation(jax.random.fold_in(key, 102), N - 1)
    rises = (1 + (order < N // 2).astype(jnp.int32)).astype(jnp.int32)
    indices = jnp.concatenate([jnp.zeros((1,), jnp.int32), jnp.cumsum(rises).astype(jnp.int32)]).astype(jnp.int32)
    valid_count = jax.random.randint(jax.random.fold_in(key, 103), (), N // 2, N)
    masks = (position < valid_count).astype(jnp.int32)
    return (chains, indices, masks)


def draw_chain_number(key, part):
    return draw_structure(key)[0]


def draw_residue_index(key, part):
    return draw_structure(key)[1]


def draw_padding_mask(key, part):
    return draw_structure(key)[2]


def draw_node_states(key, part):
    value_key = jax.random.fold_in(key, 201)
    return jnp.clip(jax.random.normal(value_key, (N, C_S), jnp.float32), -6.0, 6.0)


def draw_frames(key, part):
    turns = jax.random.normal(jax.random.fold_in(key, 301), (4, N), jnp.float32)
    turns = turns / jnp.sqrt(jnp.sum(turns * turns, axis=0, keepdims=True) + 1e-12)
    real_part = turns[0]
    first_imag = turns[1]
    second_imag = turns[2]
    third_imag = turns[3]
    entries = jnp.stack([real_part * real_part + first_imag * first_imag - second_imag * second_imag - third_imag * third_imag, 2.0 * (first_imag * second_imag - real_part * third_imag), 2.0 * (first_imag * third_imag + real_part * second_imag), 2.0 * (first_imag * second_imag + real_part * third_imag), real_part * real_part - first_imag * first_imag + second_imag * second_imag - third_imag * third_imag, 2.0 * (second_imag * third_imag - real_part * first_imag), 2.0 * (first_imag * third_imag - real_part * second_imag), 2.0 * (second_imag * third_imag + real_part * first_imag), real_part * real_part - first_imag * first_imag - second_imag * second_imag + third_imag * third_imag], axis=0)
    shifts = jnp.clip(jax.random.normal(jax.random.fold_in(key, 302), (3, N), jnp.float32), -4.0, 4.0)
    return jnp.concatenate([entries, shifts], axis=0)


def block_levels(own_key, shape, pieces, smallest, top_value):
    level = 1.0
    for dim, shards_of in pieces:
        heights = jax.random.uniform(jax.random.fold_in(jax.random.fold_in(own_key, 6), dim), (shards_of,), jnp.float32, smallest / len(pieces), top_value / len(pieces))
        level = level * jnp.repeat(jnp.exp(heights), shape[dim] // shards_of).reshape((-1,) + (1,) * (len(shape) - 1 - dim))
    return level


def noise(key, dims, spread, limit, split=(), held_as=jnp.bfloat16):
    level = block_levels(key, dims, split, -0.22, 0.18) if split else 1.0
    values = jax.random.normal(key, dims, jnp.float32) * spread * level
    return jnp.minimum(jnp.maximum(values, -limit), limit).astype(held_as)


def setup_inputs(seed: int = 0) -> dict:
    keys = jax.random.split(jax.random.key(seed), 30)
    node_states = draw_node_states(jax.random.fold_in(keys[29], 71), 0)
    frames = draw_frames(jax.random.fold_in(keys[29], 71), 0)
    edge_states = noise(keys[2], (N, N, C_Z), 1.0, 6.0, ((0, 8), (1, 4)))
    chain_number = draw_chain_number(jax.random.fold_in(keys[29], 71), 0)
    residue_index = draw_residue_index(jax.random.fold_in(keys[29], 71), 0)
    padding_mask = draw_padding_mask(jax.random.fold_in(keys[29], 71), 0)
    query_weight = noise(keys[6], (C_S, HEADS * HD), C_S ** -0.5, 0.375)
    key_weight = noise(keys[7], (C_S, HEADS * HD), C_S ** -0.5, 0.375)
    value_weight = noise(keys[8], (C_S, HEADS * HD), C_S ** -0.5, 0.375)
    point_query = noise(keys[9], (C_S, HEADS * 3 * QKP), C_S ** -0.5, 0.375)
    point_key = noise(keys[10], (C_S, HEADS * 3 * QKP), C_S ** -0.5, 0.375)
    point_value = noise(keys[11], (C_S, HEADS * 3 * VP), C_S ** -0.5, 0.375)
    bias_weight = noise(keys[12], (C_Z, HEADS), C_Z ** -0.5, 0.5)
    point_gamma = jnp.clip(jnp.exp(jax.random.uniform(keys[13], (HEADS,), jnp.float32, math.log(0.3), math.log(3.0))), 0.3, 3.0)
    relpos_table = noise(keys[14], (RELBINS, C_Z), 0.5, 3.0, (), jnp.float32)
    output_weight = noise(keys[15], (HEADS * (HD + C_Z + 4 * VP), C_S), (HEADS * (HD + C_Z + 4 * VP)) ** -0.5, 0.109375)
    attention_scales = jnp.clip(1.0 + 0.1 * jax.random.normal(keys[16], (C_S,), jnp.float32), 0.5, 1.5)
    layer_project = noise(keys[17], (LAYERS, C_S, 3 * C_S), C_S ** -0.5, 0.375)
    layer_output = noise(keys[18], (LAYERS, C_S, C_S), C_S ** -0.5, 0.375)
    layer_expand = noise(keys[19], (LAYERS, C_S, C_S), C_S ** -0.5, 0.375)
    layer_shrink = noise(keys[20], (LAYERS, C_S, C_S), C_S ** -0.5, 0.375)
    layer_scales = jnp.clip(1.0 + 0.1 * jax.random.normal(keys[21], (LAYERS, 2, C_S), jnp.float32), 0.5, 1.5)
    frame_weight = noise(keys[22], (C_S, 6), C_S ** -0.5, 0.375, (), jnp.float32)
    node_to_edge = noise(keys[23], (C_S, 2 * EH), C_S ** -0.5, 0.375)
    edge_first = noise(keys[24], (C_Z, EH), C_Z ** -0.5, 0.5)
    edge_second = noise(keys[25], (EH, EH), EH ** -0.5, 0.3125)
    edge_third = noise(keys[26], (EH, C_Z), EH ** -0.5, 0.3125)
    edge_biases = noise(keys[27], (2, EH), 0.5, 3.0, (), jnp.float32)
    edge_scales = jnp.clip(1.0 + 0.1 * jax.random.normal(keys[28], (C_Z,), jnp.float32), 0.5, 1.5)
    return dict(node_states=node_states, frames=frames, edge_states=edge_states, chain_number=chain_number, residue_index=residue_index, padding_mask=padding_mask, query_weight=query_weight, key_weight=key_weight, value_weight=value_weight, point_query=point_query, point_key=point_key, point_value=point_value, bias_weight=bias_weight, point_gamma=point_gamma, relpos_table=relpos_table, output_weight=output_weight, attention_scales=attention_scales, layer_project=layer_project, layer_output=layer_output, layer_expand=layer_expand, layer_shrink=layer_shrink, layer_scales=layer_scales, frame_weight=frame_weight, node_to_edge=node_to_edge, edge_first=edge_first, edge_second=edge_second, edge_third=edge_third, edge_biases=edge_biases, edge_scales=edge_scales)


HIGHEST = lax.Precision.HIGHEST
NEG_FILL = -1000000000.0

def layer_norm(values, scales):
    centered = values - lax.optimization_barrier(jnp.mean(values, axis=-1, keepdims=True))
    variance = lax.optimization_barrier(jnp.mean(centered * centered, axis=-1, keepdims=True))
    return centered * lax.rsqrt(variance + 1e-05) * scales

def frame_parts(frames):
    rotation = jnp.transpose(frames[:9]).reshape(-1, 3, 3)
    offset = jnp.transpose(frames[9:12])
    return (rotation, offset)

def head_split(matrix, width):
    return matrix.reshape(matrix.shape[0], -1, width)

def place_points(features, weight, rotation, offset, count):
    local = jnp.dot(features, weight, preferred_element_type=jnp.float32)
    local = local.reshape(local.shape[0], HEADS, 3, count)
    placed = jnp.einsum('rcd,rhdp->rhcp', rotation, local, precision=HIGHEST)
    return placed + offset[:, None, :, None]

def relative_bins(chain_rows, index_rows, chain_cols, index_cols):
    reach = (RELBINS - 2) // 2
    gap_class = jnp.clip(index_rows[:, None] - index_cols[None, :], -reach, reach) + reach
    same_chain = chain_rows[:, None] == chain_cols[None, :]
    return jnp.where(same_chain, gap_class, RELBINS - 1).astype(jnp.int32)

def point_logits(queries, key_vectors, query_places, key_places, pair_rep, bias_weight, point_gamma):
    scalar = jnp.einsum('ihd,jhd->hij', queries.astype(jnp.float32), key_vectors.astype(jnp.float32), precision=HIGHEST) / math.sqrt(HD)
    pair_bias = jnp.einsum('ijc,ch->hij', pair_rep.astype(jnp.float32), bias_weight.astype(jnp.float32), precision=HIGHEST)
    query_square = lax.optimization_barrier(jnp.sum(query_places * query_places, axis=(2, 3)))
    key_square = lax.optimization_barrier(jnp.sum(key_places * key_places, axis=(2, 3)))
    cross = jnp.einsum('ihcp,jhcp->hij', query_places, key_places, precision=HIGHEST)
    distance = jnp.transpose(query_square)[:, :, None] + jnp.transpose(key_square)[:, None, :] - 2.0 * cross
    weight_points = math.sqrt(2.0 / (9.0 * QKP))
    return math.sqrt(1.0 / 3.0) * (scalar + pair_bias - 0.5 * weight_points * point_gamma[:, None, None] * distance)

def ipa_features(scalar_out, pair_out, point_global, rotation, offset):
    moved = point_global - offset[:, None, :, None]
    local = jnp.einsum('icd,ihcp->ihdp', rotation, moved, precision=HIGHEST)
    lengths = jnp.sqrt(lax.optimization_barrier(jnp.sum(local * local, axis=2)) + 1e-08)
    count = scalar_out.shape[0]
    return jnp.concatenate([scalar_out.reshape(count, -1), pair_out.reshape(count, -1), local.reshape(count, -1), lengths.reshape(count, -1)], axis=1)

def encoder_core(states, query_half, key_value, valid, output, expand, shrink, scales):
    queries = head_split(query_half, TF_HD)
    key_vectors = head_split(key_value[:, :C_S], TF_HD)
    value_vectors = head_split(key_value[:, C_S:], TF_HD)
    scores = jnp.einsum('ihd,jhd->hij', queries.astype(jnp.float32), key_vectors.astype(jnp.float32), precision=HIGHEST) / math.sqrt(TF_HD)
    masked = jnp.where(valid[None, None, :], scores, NEG_FILL)
    row_top = lax.optimization_barrier(jnp.max(masked, axis=-1, keepdims=True))
    weights = jnp.where(valid[None, None, :], jnp.exp(masked - row_top), 0.0)
    attention = (weights / lax.optimization_barrier(jnp.sum(weights, axis=-1, keepdims=True))).astype(jnp.bfloat16)
    context = jnp.einsum('hij,jhd->ihd', attention.astype(jnp.float32), value_vectors.astype(jnp.float32), precision=HIGHEST).astype(jnp.bfloat16)
    context = context.reshape(states.shape[0], C_S)
    middle = layer_norm(states + jnp.dot(context, output, preferred_element_type=jnp.float32), scales[0])
    hidden = jax.nn.relu(jnp.dot(middle.astype(jnp.bfloat16), expand, preferred_element_type=jnp.float32)).astype(jnp.bfloat16)
    return layer_norm(middle + jnp.dot(hidden, shrink, preferred_element_type=jnp.float32), scales[1])

def update_frames(states, frames, frame_weight):
    update = jnp.dot(states, frame_weight, precision=HIGHEST)
    length = jnp.sqrt(1.0 + update[:, 0] * update[:, 0] + update[:, 1] * update[:, 1] + update[:, 2] * update[:, 2])
    real_part = 1.0 / length
    first_imag = update[:, 0] / length
    second_imag = update[:, 1] / length
    third_imag = update[:, 2] / length
    row_one = jnp.stack([real_part * real_part + first_imag * first_imag - second_imag * second_imag - third_imag * third_imag, 2.0 * (first_imag * second_imag - real_part * third_imag), 2.0 * (first_imag * third_imag + real_part * second_imag)], axis=1)
    row_two = jnp.stack([2.0 * (first_imag * second_imag + real_part * third_imag), real_part * real_part - first_imag * first_imag + second_imag * second_imag - third_imag * third_imag, 2.0 * (second_imag * third_imag - real_part * first_imag)], axis=1)
    row_three = jnp.stack([2.0 * (first_imag * third_imag - real_part * second_imag), 2.0 * (second_imag * third_imag + real_part * first_imag), real_part * real_part - first_imag * first_imag - second_imag * second_imag + third_imag * third_imag], axis=1)
    turn = jnp.stack([row_one, row_two, row_three], axis=1)
    rotation, offset = frame_parts(frames)
    new_rotation = jnp.einsum('rcd,rde->rce', rotation, turn, precision=HIGHEST)
    new_offset = jnp.einsum('rcd,rd->rc', rotation, update[:, 3:6], precision=HIGHEST) + offset
    return jnp.transpose(jnp.concatenate([new_rotation.reshape(-1, 9), new_offset], axis=1))

def rows_of(array, row_first):
    return lax.dynamic_slice_in_dim(array, row_first, QD, 0)

def reference(node_states, frames, edge_states, chain_number, residue_index, padding_mask, query_weight, key_weight, value_weight, point_query, point_key, point_value, bias_weight, point_gamma, relpos_table, output_weight, attention_scales, layer_project, layer_output, layer_expand, layer_shrink, layer_scales, frame_weight, node_to_edge, edge_first, edge_second, edge_third, edge_biases, edge_scales):
    rotation, offset = frame_parts(frames)
    rounded = node_states.astype(jnp.bfloat16)
    queries = head_split(jnp.dot(rounded, query_weight, preferred_element_type=jnp.float32).astype(jnp.bfloat16), HD)
    key_vectors = head_split(jnp.dot(rounded, key_weight, preferred_element_type=jnp.float32).astype(jnp.bfloat16), HD)
    value_vectors = head_split(jnp.dot(rounded, value_weight, preferred_element_type=jnp.float32).astype(jnp.bfloat16), HD)
    query_places = place_points(rounded, point_query, rotation, offset, QKP)
    key_places = place_points(rounded, point_key, rotation, offset, QKP)
    value_places = place_points(rounded, point_value, rotation, offset, VP)
    valid = padding_mask == 1
    live_float = valid.astype(jnp.float32)
    starts = jnp.arange(N_PB, dtype=jnp.int32) * QD

    def pair_rows(row_first):
        edge_rows = rows_of(edge_states, row_first)
        bins = relative_bins(rows_of(chain_number, row_first), rows_of(residue_index, row_first), chain_number, residue_index)
        relative = jnp.take(relpos_table, bins, axis=0)
        return (edge_rows.astype(jnp.float32) + relative).astype(jnp.bfloat16)

    def attend_rows(row_first):
        pair_rep = pair_rows(row_first)
        logits = point_logits(rows_of(queries, row_first), key_vectors, rows_of(query_places, row_first), key_places, pair_rep, bias_weight, point_gamma)
        masked = jnp.where(valid[None, None, :], logits, NEG_FILL)
        row_top = lax.optimization_barrier(jnp.max(masked, axis=-1, keepdims=True))
        weights = jnp.where(valid[None, None, :], jnp.exp(masked - row_top), 0.0)
        attention = weights / lax.optimization_barrier(jnp.sum(weights, axis=-1, keepdims=True))
        scalar_out = jnp.einsum('hij,jhd->ihd', attention, value_vectors.astype(jnp.float32), precision=HIGHEST)
        pair_out = jnp.einsum('hij,ijc->ihc', attention, pair_rep.astype(jnp.float32), precision=HIGHEST)
        point_global = jnp.einsum('hij,jhcp->ihcp', attention, value_places, precision=HIGHEST)
        return ipa_features(scalar_out, pair_out, point_global, rows_of(rotation, row_first), rows_of(offset, row_first))
    features = lax.map(attend_rows, starts)
    features = features.reshape(N, -1).astype(jnp.bfloat16)
    states = layer_norm(node_states + jnp.dot(features, output_weight, preferred_element_type=jnp.float32), attention_scales)
    for layer_number in range(LAYERS):
        projected = jnp.dot(states.astype(jnp.bfloat16), layer_project[layer_number], preferred_element_type=jnp.float32).astype(jnp.bfloat16)
        states = encoder_core(states, projected[:, :C_S], projected[:, C_S:], valid, layer_output[layer_number], layer_expand[layer_number], layer_shrink[layer_number], layer_scales[layer_number])
    frames_out = update_frames(states, frames, frame_weight)
    edge_projection = jnp.dot(states.astype(jnp.bfloat16), node_to_edge, preferred_element_type=jnp.float32)

    def edge_rows_update(row_first):
        pair_rep = pair_rows(row_first)
        query_part = rows_of(edge_projection, row_first)[:, :EH]
        hidden = jnp.dot(pair_rep.reshape(-1, C_Z), edge_first, preferred_element_type=jnp.float32).reshape(QD, N, EH)
        hidden = jax.nn.relu(hidden + query_part[:, None, :] + edge_projection[None, :, EH:] + edge_biases[0]).astype(jnp.bfloat16)
        middle = jax.nn.relu(jnp.dot(hidden.reshape(-1, EH), edge_second, preferred_element_type=jnp.float32) + edge_biases[1]).astype(jnp.bfloat16)
        result = pair_rep.astype(jnp.float32) + jnp.dot(middle, edge_third, preferred_element_type=jnp.float32).reshape(QD, N, C_Z)
        live = rows_of(live_float, row_first)[:, None, None] * live_float[None, :, None]
        return (layer_norm(result, edge_scales) * live).astype(jnp.bfloat16)
    edges_out = lax.map(edge_rows_update, starts).reshape(N, N, C_Z)
    return (states, frames_out, edges_out)
```

```python
import functools
import math

import jax
import jax.numpy as jnp
from jax import lax
from jax.experimental import pallas as pl
from jax.experimental.pallas import tpu as pltpu
from jax.sharding import PartitionSpec as P

C_S = 256
HEADS = 8
HD = 256
QKP = 8
VP = 12
EH = 384
RELBINS = 128
LAYERS = 2
TF_HD = 64


HIGHEST = lax.Precision.HIGHEST
NEG_FILL = -1000000000.0


def layer_norm(values, scales):
    centered = values - jnp.mean(values, axis=-1, keepdims=True)
    variance = jnp.mean(centered * centered, axis=-1, keepdims=True)
    return centered * lax.rsqrt(variance + 1e-05) * scales


def frame_parts(frames):
    rotation = jnp.transpose(frames[:9]).reshape(-1, 3, 3)
    offset = jnp.transpose(frames[9:12])
    return (rotation, offset)


def head_split(matrix, width):
    return matrix.reshape(matrix.shape[0], -1, width)


def place_points(features, weight, rotation, offset, count):
    local = jnp.dot(features, weight, preferred_element_type=jnp.float32)
    local = local.reshape(local.shape[0], HEADS, 3, count)
    placed = jnp.einsum("rcd,rhdp->rhcp", rotation, local, precision=HIGHEST)
    return placed + offset[:, None, :, None]


def relative_bins(chain_rows, index_rows, chain_cols, index_cols):
    reach = (RELBINS - 2) // 2
    gap_class = jnp.clip(index_rows[:, None] - index_cols[None, :], -reach, reach) + reach
    same_chain = chain_rows[:, None] == chain_cols[None, :]
    return jnp.where(same_chain, gap_class, RELBINS - 1)


def point_logits(
    queries, key_vectors, query_places, key_places, pair_rep, bias_weight, point_gamma
):
    scalar = jnp.einsum(
        "ihd,jhd->hij", queries, key_vectors, preferred_element_type=jnp.float32
    ) / math.sqrt(HD)
    pair_bias = jnp.einsum("ijc,ch->hij", pair_rep, bias_weight, preferred_element_type=jnp.float32)
    query_square = jnp.sum(query_places * query_places, axis=(2, 3))
    key_square = jnp.sum(key_places * key_places, axis=(2, 3))
    cross = jnp.einsum("ihcp,jhcp->hij", query_places, key_places, precision=HIGHEST)
    distance = (
        jnp.transpose(query_square)[:, :, None]
        + jnp.transpose(key_square)[:, None, :]
        - 2.0 * cross
    )
    weight_points = math.sqrt(2.0 / (9.0 * QKP))
    return math.sqrt(1.0 / 3.0) * (
        scalar + pair_bias - 0.5 * weight_points * point_gamma[:, None, None] * distance
    )


def ipa_features(scalar_out, pair_out, point_global, rotation, offset):
    moved = point_global - offset[:, None, :, None]
    local = jnp.einsum("icd,ihcp->ihdp", rotation, moved, precision=HIGHEST)
    lengths = jnp.sqrt(jnp.sum(local * local, axis=2) + 1e-08)
    count = scalar_out.shape[0]
    return jnp.concatenate(
        [
            scalar_out.reshape(count, -1),
            pair_out.reshape(count, -1),
            local.reshape(count, -1),
            lengths.reshape(count, -1),
        ],
        axis=1,
    )


def encoder_core(states, query_half, key_value, valid, output, expand, shrink, scales):
    queries = head_split(query_half, TF_HD)
    key_vectors = head_split(key_value[:, :C_S], TF_HD)
    value_vectors = head_split(key_value[:, C_S:], TF_HD)
    scores = jnp.einsum(
        "ihd,jhd->hij", queries, key_vectors, preferred_element_type=jnp.float32
    ) / math.sqrt(TF_HD)
    masked = jnp.where(valid[None, None, :], scores, NEG_FILL)
    row_top = jnp.max(masked, axis=-1, keepdims=True)
    weights = jnp.where(valid[None, None, :], jnp.exp(masked - row_top), 0.0)
    attention = (weights / jnp.sum(weights, axis=-1, keepdims=True)).astype(jnp.bfloat16)
    context = jnp.einsum(
        "hij,jhd->ihd", attention, value_vectors, preferred_element_type=jnp.float32
    ).astype(jnp.bfloat16)
    context = context.reshape(states.shape[0], C_S)
    middle = layer_norm(
        states + jnp.dot(context, output, preferred_element_type=jnp.float32), scales[0]
    )
    hidden = jax.nn.relu(
        jnp.dot(middle.astype(jnp.bfloat16), expand, preferred_element_type=jnp.float32)
    ).astype(jnp.bfloat16)
    return layer_norm(
        middle + jnp.dot(hidden, shrink, preferred_element_type=jnp.float32), scales[1]
    )


def update_frames(states, frames, frame_weight):
    update = jnp.dot(states, frame_weight, precision=HIGHEST)
    length = jnp.sqrt(
        1.0
        + update[:, 0] * update[:, 0]
        + update[:, 1] * update[:, 1]
        + update[:, 2] * update[:, 2]
    )
    real_part = 1.0 / length
    first_imag = update[:, 0] / length
    second_imag = update[:, 1] / length
    third_imag = update[:, 2] / length
    row_one = jnp.stack(
        [
            real_part * real_part
            + first_imag * first_imag
            - second_imag * second_imag
            - third_imag * third_imag,
            2.0 * (first_imag * second_imag - real_part * third_imag),
            2.0 * (first_imag * third_imag + real_part * second_imag),
        ],
        axis=1,
    )
    row_two = jnp.stack(
        [
            2.0 * (first_imag * second_imag + real_part * third_imag),
            real_part * real_part
            - first_imag * first_imag
            + second_imag * second_imag
            - third_imag * third_imag,
            2.0 * (second_imag * third_imag - real_part * first_imag),
        ],
        axis=1,
    )
    row_three = jnp.stack(
        [
            2.0 * (first_imag * third_imag - real_part * second_imag),
            2.0 * (second_imag * third_imag + real_part * first_imag),
            real_part * real_part
            - first_imag * first_imag
            - second_imag * second_imag
            + third_imag * third_imag,
        ],
        axis=1,
    )
    turn = jnp.stack([row_one, row_two, row_three], axis=1)
    rotation, offset = frame_parts(frames)
    new_rotation = jnp.einsum("rcd,rde->rce", rotation, turn, precision=HIGHEST)
    new_offset = jnp.einsum("rcd,rd->rc", rotation, update[:, 3:6], precision=HIGHEST) + offset
    return jnp.transpose(jnp.concatenate([new_rotation.reshape(-1, 9), new_offset], axis=1))


MESH = pl.DeviceIdType.MESH


def greet(peers):
    barrier = pltpu.get_barrier_semaphore()
    for peer in peers:
        pl.semaphore_signal(barrier, inc=1, device_id=peer, device_id_type=MESH)
    pl.semaphore_wait(barrier, len(peers))


def key_tile_kernel(n_pb, n_ka, x_ref, o_ref, send, recv, own):
    row, col = lax.axis_index("pb"), lax.axis_index("ka")
    per = n_pb // n_ka
    peers = [{"pb": lax.rem(row + d, n_pb)} for d in range(1, n_pb)]
    greet(peers)
    for slot in range(per):

        @pl.when(row == col * per + slot)
        def _():
            local = pltpu.make_async_copy(x_ref, o_ref.at[slot], own)
            local.start()
            copies = [
                pltpu.make_async_remote_copy(
                    src_ref=x_ref,
                    dst_ref=o_ref.at[slot],
                    send_sem=send.at[d],
                    recv_sem=recv.at[slot],
                    device_id=peer,
                    device_id_type=MESH,
                )
                for d, peer in enumerate(peers)
            ]
            for copy in copies:
                copy.start()
            for copy in copies:
                copy.wait_send()
            local.wait()

    for slot in range(per):

        @pl.when(row != col * per + slot)
        def _():
            pltpu.make_async_remote_copy(
                src_ref=x_ref,
                dst_ref=o_ref.at[slot],
                send_sem=send.at[0],
                recv_sem=recv.at[slot],
                device_id=peers[0],
                device_id_type=MESH,
            ).wait_recv()


def key_tile(packed, n_pb, n_ka):
    per = n_pb // n_ka
    return pl.pallas_call(
        functools.partial(key_tile_kernel, n_pb, n_ka),
        out_shape=jax.ShapeDtypeStruct((per,) + packed.shape, packed.dtype),
        in_specs=[pl.BlockSpec(memory_space=pltpu.VMEM)],
        out_specs=pl.BlockSpec(memory_space=pltpu.VMEM),
        scratch_shapes=[
            pltpu.SemaphoreType.DMA((n_pb - 1,)),
            pltpu.SemaphoreType.DMA((per,)),
            pltpu.SemaphoreType.DMA,
        ],
        compiler_params=pltpu.CompilerParams(collective_id=0, has_side_effects=True),
    )(packed)


def exchange_kernel(n_ka, sums_ref, stats_ref, sums_out, stats_out, send, recv, own):
    me = lax.axis_index("ka")
    peers = [lax.rem(me + d, n_ka) for d in range(1, n_ka)]
    greet([{"ka": peer} for peer in peers])
    copies = []
    for d, peer in enumerate(peers):
        for part, (source, target) in enumerate(((sums_ref, sums_out), (stats_ref, stats_out))):
            copy = pltpu.make_async_remote_copy(
                src_ref=source.at[peer],
                dst_ref=target.at[me],
                send_sem=send.at[2 * d + part],
                recv_sem=recv.at[2 * d + part],
                device_id={"ka": peer},
                device_id_type=MESH,
            )
            copy.start()
            copies.append(copy)
    for part, (source, target) in enumerate(((sums_ref, sums_out), (stats_ref, stats_out))):
        copy = pltpu.make_async_copy(source.at[me], target.at[me], own.at[part])
        copy.start()
        copies.append(copy)
    for copy in copies:
        copy.wait()


def exchange(sums, stats, n_ka):
    return pl.pallas_call(
        functools.partial(exchange_kernel, n_ka),
        out_shape=(
            jax.ShapeDtypeStruct(sums.shape, sums.dtype),
            jax.ShapeDtypeStruct(stats.shape, stats.dtype),
        ),
        in_specs=[pl.BlockSpec(memory_space=pltpu.VMEM)] * 2,
        out_specs=(pl.BlockSpec(memory_space=pltpu.VMEM),) * 2,
        scratch_shapes=[
            pltpu.SemaphoreType.DMA((2 * n_ka - 2,)),
            pltpu.SemaphoreType.DMA((2 * n_ka - 2,)),
            pltpu.SemaphoreType.DMA((2,)),
        ],
        compiler_params=pltpu.CompilerParams(collective_id=1, has_side_effects=True),
    )(sums, stats)


def gather_kernel(n_pb, n_ka, x_ref, o_ref, send, recv, own):
    row, col = lax.axis_index("pb"), lax.axis_index("ka")
    along_pb = [{"pb": lax.rem(row + d, n_pb)} for d in range(1, n_pb)]
    along_ka = [{"ka": lax.rem(col + d, n_ka)} for d in range(1, n_ka)]
    greet(along_pb + along_ka)
    copies = [pltpu.make_async_copy(x_ref, o_ref.at[col, row], own)] + [
        pltpu.make_async_remote_copy(
            src_ref=x_ref,
            dst_ref=o_ref.at[col, row],
            send_sem=send.at[d],
            recv_sem=recv.at[d],
            device_id=peer,
            device_id_type=MESH,
        )
        for d, peer in enumerate(along_pb)
    ]
    for copy in copies:
        copy.start()
    for copy in copies:
        copy.wait()
    copies = [
        pltpu.make_async_remote_copy(
            src_ref=o_ref.at[col],
            dst_ref=o_ref.at[col],
            send_sem=send.at[n_pb - 1 + d],
            recv_sem=recv.at[n_pb - 1 + d],
            device_id=peer,
            device_id_type=MESH,
        )
        for d, peer in enumerate(along_ka)
    ]
    for copy in copies:
        copy.start()
    for copy in copies:
        copy.wait()


def gather_rows(x, n_pb, n_ka):
    out = pl.pallas_call(
        functools.partial(gather_kernel, n_pb, n_ka),
        out_shape=jax.ShapeDtypeStruct((n_ka, n_pb) + x.shape, x.dtype),
        in_specs=[pl.BlockSpec(memory_space=pltpu.VMEM)],
        out_specs=pl.BlockSpec(memory_space=pltpu.VMEM),
        scratch_shapes=[
            pltpu.SemaphoreType.DMA((n_pb + n_ka - 2,)),
            pltpu.SemaphoreType.DMA((n_pb + n_ka - 2,)),
            pltpu.SemaphoreType.DMA,
        ],
        compiler_params=pltpu.CompilerParams(collective_id=2, has_side_effects=True),
    )(x)
    return jnp.transpose(out, (1, 0, 2, 3)).reshape(-1, x.shape[-1])


def edge_kernel(
    pair_ref, row_ref, key_ref, live_row, live_key, first, second, third, bias, scale, o_ref
):
    rows, keys, width = pair_ref.shape
    pair = pair_ref[...].reshape(rows * keys, width)
    hidden = jnp.dot(pair, first[...], preferred_element_type=jnp.float32)
    hidden = hidden.reshape(rows, keys, -1) + row_ref[...][:, None, :] + key_ref[...][None]
    hidden = jnp.maximum(hidden, 0.0).astype(jnp.bfloat16).reshape(rows * keys, -1)
    middle = jnp.dot(hidden, second[...], preferred_element_type=jnp.float32) + bias[...]
    middle = jnp.maximum(middle, 0.0).astype(jnp.bfloat16)
    result = pair.astype(jnp.float32) + jnp.dot(
        middle, third[...], preferred_element_type=jnp.float32
    )
    normed = layer_norm(result, scale[...]).reshape(rows, keys, width)
    live = live_row[...][:, None, :] * live_key[...][None]
    o_ref[...] = (normed * live).astype(o_ref.dtype)


def edge_transition(pair_rep, row_part, key_part, mask_rows, mask_keys, mats, bias, scale):
    rows, keys, width = pair_rep.shape
    step = 8
    live_row = jnp.broadcast_to(mask_rows.astype(jnp.float32)[:, None], (rows, width))
    live_key = jnp.broadcast_to(mask_keys.astype(jnp.float32)[:, None], (keys, width))

    def whole(array):
        return pl.BlockSpec(array.shape, lambda i: (0, 0))

    flat = [live_key, *mats, bias[None], scale[None]]
    return pl.pallas_call(
        edge_kernel,
        grid=(rows // step,),
        out_shape=jax.ShapeDtypeStruct(pair_rep.shape, jnp.bfloat16),
        in_specs=[
            pl.BlockSpec((step, keys, width), lambda i: (i, 0, 0)),
            pl.BlockSpec((step, row_part.shape[1]), lambda i: (i, 0)),
            whole(key_part),
            pl.BlockSpec((step, width), lambda i: (i, 0)),
        ]
        + [whole(array) for array in flat],
        out_specs=pl.BlockSpec((step, keys, width), lambda i: (i, 0, 0)),
    )(pair_rep, row_part, key_part, live_row, *flat)


def finish_rows(
    row_total,
    scalar_acc,
    pair_acc,
    point_acc,
    rotation,
    offset,
    states,
    output_weight,
    attention_scales,
):
    inverse = 1.0 / row_total
    scalar_out = scalar_acc * inverse[..., None]
    pair_out = pair_acc * inverse[..., None]
    point_global = point_acc * inverse[..., None, None]
    features = ipa_features(scalar_out, pair_out, point_global, rotation, offset).astype(
        jnp.bfloat16
    )
    return layer_norm(
        states + jnp.dot(features, output_weight, preferred_element_type=jnp.float32),
        attention_scales,
    )


def on_device(
    node_states,
    frames,
    edge_states,
    chain_number,
    residue_index,
    padding_mask,
    query_weight,
    key_weight,
    value_weight,
    point_query,
    point_key,
    point_value,
    bias_weight,
    point_gamma,
    relpos_table,
    output_weight,
    attention_scales,
    layer_project,
    layer_output,
    layer_expand,
    layer_shrink,
    layer_scales,
    frame_weight,
    node_to_edge,
    edge_first,
    edge_second,
    edge_third,
    edge_biases,
    edge_scales,
):
    row_count = node_states.shape[0]
    key_count = edge_states.shape[1]
    row_first = lax.axis_index("pb") * row_count
    key_first = lax.axis_index("ka") * key_count
    n_pb, n_ka = lax.axis_size("pb"), lax.axis_size("ka")
    packed = jnp.concatenate([node_states, jnp.transpose(frames)], axis=1).astype(jnp.bfloat16)
    packed = jnp.pad(packed, ((0, 0), (0, -packed.shape[1] % 128)))
    tile = key_tile(packed, n_pb, n_ka).reshape(key_count, -1)
    key_input = tile[:, :C_S]
    key_frames = jnp.transpose(tile[:, C_S : C_S + 12].astype(jnp.float32))
    chain_rows = lax.dynamic_slice_in_dim(chain_number, row_first, row_count, 0)
    chain_keys = lax.dynamic_slice_in_dim(chain_number, key_first, key_count, 0)
    index_rows = lax.dynamic_slice_in_dim(residue_index, row_first, row_count, 0)
    index_keys = lax.dynamic_slice_in_dim(residue_index, key_first, key_count, 0)
    mask_rows = lax.dynamic_slice_in_dim(padding_mask, row_first, row_count, 0)
    mask_keys = lax.dynamic_slice_in_dim(padding_mask, key_first, key_count, 0)
    rotation, offset = frame_parts(frames)
    key_rotation, key_offset = frame_parts(key_frames)
    row_input = node_states.astype(jnp.bfloat16)
    queries = head_split(
        jnp.dot(row_input, query_weight, preferred_element_type=jnp.float32).astype(jnp.bfloat16),
        HD,
    )
    key_vectors = head_split(
        jnp.dot(key_input, key_weight, preferred_element_type=jnp.float32).astype(jnp.bfloat16), HD
    )
    value_vectors = head_split(
        jnp.dot(key_input, value_weight, preferred_element_type=jnp.float32).astype(jnp.bfloat16),
        HD,
    )
    query_places = place_points(row_input, point_query, rotation, offset, QKP)
    key_places = place_points(key_input, point_key, key_rotation, key_offset, QKP)
    value_places = place_points(key_input, point_value, key_rotation, key_offset, VP)
    bins = relative_bins(chain_rows, index_rows, chain_keys, index_keys)
    onehot = (bins[:, :, None] == jnp.arange(RELBINS, dtype=jnp.int32)).astype(jnp.float32)
    relative = jnp.dot(onehot.reshape(-1, RELBINS), relpos_table, precision=HIGHEST).reshape(
        row_count, key_count, -1
    )
    pair_rep = (edge_states.astype(jnp.float32) + relative).astype(jnp.bfloat16)
    logits = point_logits(
        queries, key_vectors, query_places, key_places, pair_rep, bias_weight, point_gamma
    )
    key_valid = (mask_keys == 1)[None, None, :]
    masked = jnp.where(key_valid, logits, NEG_FILL)
    local_top = jnp.max(masked, axis=-1)
    weights = jnp.where(key_valid, jnp.exp(masked - local_top[..., None]), 0.0)
    local_total = jnp.sum(weights, axis=-1)
    scalar_acc = jnp.einsum(
        "hij,jhd->hid", weights, value_vectors.astype(jnp.float32), precision=HIGHEST
    )
    pair_acc = jnp.einsum("hij,ijc->hic", weights, pair_rep.astype(jnp.float32), precision=HIGHEST)
    point_acc = jnp.einsum("hij,jhcp->hicp", weights, value_places, precision=HIGHEST)
    part = row_count // n_ka
    sums = jnp.concatenate(
        [
            jnp.transpose(scalar_acc, (1, 0, 2)).reshape(row_count, -1),
            jnp.transpose(pair_acc, (1, 0, 2)).reshape(row_count, -1),
            jnp.transpose(point_acc, (1, 0, 2, 3)).reshape(row_count, -1),
        ],
        axis=1,
    ).astype(jnp.bfloat16)
    used = sums.shape[1]
    sums = jnp.pad(sums, ((0, 0), (0, -used % 128))).reshape(n_ka, part, -1)
    stats = jnp.concatenate([jnp.transpose(local_top), jnp.transpose(local_total)], axis=1)
    stats = jnp.pad(stats, ((0, 0), (0, -stats.shape[1] % 128))).reshape(n_ka, part, -1)
    sums, stats = exchange(sums, stats, n_ka)
    tops, totals = stats[..., :HEADS], stats[..., HEADS : 2 * HEADS]
    factor = jnp.exp(tops - jnp.max(tops, axis=0))
    row_total = jnp.sum(totals * factor, axis=0)
    channels = pair_rep.shape[-1]
    ends = (HEADS * HD, HEADS * (HD + channels))
    spread = jnp.concatenate(
        [
            jnp.repeat(factor, HD, axis=2),
            jnp.repeat(factor, channels, axis=2),
            jnp.repeat(factor, 3 * VP, axis=2),
        ],
        axis=2,
    )
    merged = jnp.sum(sums[..., :used].astype(jnp.float32) * spread, axis=0)
    part_first = lax.axis_index("ka") * part
    first_states = finish_rows(
        row_total,
        merged[:, : ends[0]].reshape(part, HEADS, HD),
        merged[:, ends[0] : ends[1]].reshape(part, HEADS, channels),
        merged[:, ends[1] :].reshape(part, HEADS, 3, VP),
        lax.dynamic_slice_in_dim(rotation, part_first, part, 0),
        lax.dynamic_slice_in_dim(offset, part_first, part, 0),
        lax.dynamic_slice_in_dim(node_states, part_first, part, 0),
        output_weight,
        attention_scales,
    )
    every_valid = padding_mask == 1
    whole_states = gather_rows(first_states.astype(jnp.bfloat16), n_pb, n_ka).astype(
        first_states.dtype
    )
    for layer_number in range(LAYERS):
        projected = jnp.dot(
            whole_states.astype(jnp.bfloat16),
            layer_project[layer_number],
            preferred_element_type=jnp.float32,
        ).astype(jnp.bfloat16)
        whole_states = encoder_core(
            whole_states,
            projected[:, :C_S],
            projected[:, C_S:],
            every_valid,
            layer_output[layer_number],
            layer_expand[layer_number],
            layer_shrink[layer_number],
            layer_scales[layer_number],
        )
    second_states = lax.dynamic_slice_in_dim(whole_states, row_first, row_count, 0)
    key_second = lax.dynamic_slice_in_dim(whole_states, key_first, key_count, 0)
    frames_out = update_frames(second_states, frames, frame_weight)
    row_project = jnp.dot(
        second_states.astype(jnp.bfloat16), node_to_edge[:, :EH], preferred_element_type=jnp.float32
    )
    key_project = jnp.dot(
        key_second.astype(jnp.bfloat16), node_to_edge[:, EH:], preferred_element_type=jnp.float32
    )
    edges_out = edge_transition(
        pair_rep,
        row_project,
        key_project + edge_biases[0],
        mask_rows,
        mask_keys,
        (edge_first, edge_second, edge_third),
        edge_biases[1],
        edge_scales,
    )
    return (second_states, frames_out, edges_out)


def solution(mesh):
    placed = (
        P("pb", None),
        P(None, "pb"),
        P("pb", "ka", None),
        P(),
        P(),
        P(),
        P(),
        P(),
        P(),
        P(),
        P(),
        P(),
        P(),
        P(),
        P(),
        P(),
        P(),
        P(),
        P(),
        P(),
        P(),
        P(),
        P(),
        P(),
        P(),
        P(),
        P(),
        P(),
        P(),
    )
    return jax.shard_map(
        on_device,
        mesh=mesh,
        in_specs=placed,
        out_specs=(P("pb", None), P(None, "pb"), P("pb", "ka", None)),
        check_vma=False,
    )
```

```python
import functools
import math

import jax
import jax.numpy as jnp
import numpy as np
from jax import lax
from jax.experimental import pallas as pl
from jax.experimental.pallas import tpu as pltpu
from jax.sharding import PartitionSpec as P

C_S = 256
HEADS = 8
HD = 256
QKP = 8
VP = 12
EH = 384
RELBINS = 128
LAYERS = 2
TF_HD = 64


HIGHEST = lax.Precision.HIGHEST
NEG_FILL = -1000000000.0


def layer_norm(values, scales):
    centered = values - jnp.mean(values, axis=-1, keepdims=True)
    variance = jnp.mean(centered * centered, axis=-1, keepdims=True)
    return centered * lax.rsqrt(variance + 1e-05) * scales


def frame_parts(frames):
    rotation = jnp.transpose(frames[:9]).reshape(-1, 3, 3)
    offset = jnp.transpose(frames[9:12])
    return (rotation, offset)


def head_split(matrix, width):
    return matrix.reshape(matrix.shape[0], -1, width)


def lane_parts(count):
    width = HEADS * 3 * count
    padded = -(-width // 128) * 128
    lane = np.arange(padded)
    real = lane < width
    head, comp, point = lane // (3 * count), lane // count % 3, lane % count
    return padded, real, head, comp, point


def pick(sources, size, dtype):
    sources = jnp.asarray(sources, jnp.int32)
    return (jnp.arange(size, dtype=jnp.int32)[:, None] == sources[None, :]).astype(dtype)


def component_copies(count, size, dtype):
    padded, real, head, comp, point = lane_parts(count)
    copies = [np.where(real, (head * 3 + d) * count + point, -1) for d in range(3)]
    return pick(np.concatenate(copies), size, dtype)


def rotation_lanes(rotation, count, inverse):
    padded, real, head, comp, point = lane_parts(count)
    entries = [np.where(real, d * 3 + comp if inverse else comp * 3 + d, -1) for d in range(3)]
    return jnp.dot(
        rotation, pick(np.concatenate(entries), 9, jnp.float32), precision=HIGHEST
    )


def offset_lanes(offset, count):
    padded, real, head, comp, point = lane_parts(count)
    return jnp.dot(offset, pick(np.where(real, comp, -1), 3, jnp.float32), precision=HIGHEST)


def head_lanes(count):
    padded, real, head, comp, point = lane_parts(count)
    return pick(np.where(real, head, -1), HEADS, jnp.float32)


def add_thirds(values):
    third = values.shape[1] // 3
    return values[:, :third] + values[:, third : 2 * third] + values[:, 2 * third :]


def place_points(features, weight, rotation, offset, count):
    copies = component_copies(count, weight.shape[1], weight.dtype)
    spread = jnp.dot(weight, copies, preferred_element_type=jnp.float32).astype(weight.dtype)
    local = jnp.dot(features, spread, preferred_element_type=jnp.float32)
    return add_thirds(local * rotation_lanes(rotation, count, False)) + offset_lanes(offset, count)


def relative_bins(chain_rows, index_rows, chain_cols, index_cols):
    reach = (RELBINS - 2) // 2
    gap_class = jnp.clip(index_rows[:, None] - index_cols[None, :], -reach, reach) + reach
    same_chain = chain_rows[:, None] == chain_cols[None, :]
    return jnp.where(same_chain, gap_class, RELBINS - 1)


def point_logits(
    queries, key_vectors, query_places, key_places, pair_rep, bias_weight, point_gamma
):
    scalar = jnp.einsum(
        "ihd,jhd->hij", queries, key_vectors, preferred_element_type=jnp.float32
    ) / math.sqrt(HD)
    pair_bias = jnp.einsum("ijc,ch->hij", pair_rep, bias_weight, preferred_element_type=jnp.float32)
    heads = head_lanes(QKP)
    query_square = lax.dot_general(
        heads, query_places * query_places, (((1,), (1,)), ((), ())), precision=HIGHEST
    )
    key_square = lax.dot_general(
        heads, key_places * key_places, (((1,), (1,)), ((), ())), precision=HIGHEST
    )
    by_head = (query_places[None] * heads[:, None, :]).reshape(-1, query_places.shape[1])
    cross = lax.dot_general(
        by_head, key_places, (((1,), (1,)), ((), ())), precision=HIGHEST
    ).reshape(HEADS, query_places.shape[0], -1)
    distance = query_square[:, :, None] + key_square[:, None, :] - 2.0 * cross
    weight_points = math.sqrt(2.0 / (9.0 * QKP))
    return math.sqrt(1.0 / 3.0) * (
        scalar + pair_bias - 0.5 * weight_points * point_gamma[:, None, None] * distance
    )


def ipa_features(merged, rotation, offset):
    points_first = merged.shape[1] - HEADS * 3 * VP
    padded, real, head, comp, point = lane_parts(VP)
    point_global = jnp.pad(
        merged[:, points_first:], ((0, 0), (0, padded - HEADS * 3 * VP))
    )
    moved = point_global - offset_lanes(offset, VP)
    rotated = jnp.dot(
        moved, component_copies(VP, padded, jnp.float32), precision=HIGHEST
    ) * rotation_lanes(rotation, VP, True)
    local = add_thirds(rotated)
    owner = np.where(real, head * VP + point, -1)
    same = jnp.transpose(pick(owner, HEADS * VP, jnp.float32))
    lengths = jnp.sqrt(jnp.dot(local * local, same, precision=HIGHEST) + 1e-08)
    return jnp.concatenate(
        [merged[:, :points_first], local[:, : HEADS * 3 * VP], lengths], axis=1
    )


def encoder_core(states, query_half, key_value, valid, output, expand, shrink, scales):
    queries = head_split(query_half, TF_HD)
    key_vectors = head_split(key_value[:, :C_S], TF_HD)
    value_vectors = head_split(key_value[:, C_S:], TF_HD)
    scores = jnp.einsum(
        "ihd,jhd->hij", queries, key_vectors, preferred_element_type=jnp.float32
    ) / math.sqrt(TF_HD)
    masked = jnp.where(valid[None, None, :], scores, NEG_FILL)
    row_top = jnp.max(masked, axis=-1, keepdims=True)
    weights = jnp.where(valid[None, None, :], jnp.exp(masked - row_top), 0.0)
    attention = (weights / jnp.sum(weights, axis=-1, keepdims=True)).astype(jnp.bfloat16)
    context = jnp.einsum(
        "hij,jhd->ihd", attention, value_vectors, preferred_element_type=jnp.float32
    ).astype(jnp.bfloat16)
    context = context.reshape(states.shape[0], C_S)
    middle = layer_norm(
        states + jnp.dot(context, output, preferred_element_type=jnp.float32), scales[0]
    )
    hidden = jax.nn.relu(
        jnp.dot(middle.astype(jnp.bfloat16), expand, preferred_element_type=jnp.float32)
    ).astype(jnp.bfloat16)
    return layer_norm(
        middle + jnp.dot(hidden, shrink, preferred_element_type=jnp.float32), scales[1]
    )


def update_frames(states, frames, frame_weight):
    update = jnp.dot(states, frame_weight, precision=HIGHEST)
    length = jnp.sqrt(
        1.0
        + update[:, 0] * update[:, 0]
        + update[:, 1] * update[:, 1]
        + update[:, 2] * update[:, 2]
    )
    real_part = 1.0 / length
    first_imag = update[:, 0] / length
    second_imag = update[:, 1] / length
    third_imag = update[:, 2] / length
    row_one = jnp.stack(
        [
            real_part * real_part
            + first_imag * first_imag
            - second_imag * second_imag
            - third_imag * third_imag,
            2.0 * (first_imag * second_imag - real_part * third_imag),
            2.0 * (first_imag * third_imag + real_part * second_imag),
        ],
        axis=1,
    )
    row_two = jnp.stack(
        [
            2.0 * (first_imag * second_imag + real_part * third_imag),
            real_part * real_part
            - first_imag * first_imag
            + second_imag * second_imag
            - third_imag * third_imag,
            2.0 * (second_imag * third_imag - real_part * first_imag),
        ],
        axis=1,
    )
    row_three = jnp.stack(
        [
            2.0 * (first_imag * third_imag - real_part * second_imag),
            2.0 * (second_imag * third_imag + real_part * first_imag),
            real_part * real_part
            - first_imag * first_imag
            - second_imag * second_imag
            + third_imag * third_imag,
        ],
        axis=1,
    )
    turn = jnp.stack([row_one, row_two, row_three], axis=1)
    rotation, offset = frame_parts(frames)
    new_rotation = jnp.einsum("rcd,rde->rce", rotation, turn, precision=HIGHEST)
    new_offset = jnp.einsum("rcd,rd->rc", rotation, update[:, 3:6], precision=HIGHEST) + offset
    return jnp.transpose(jnp.concatenate([new_rotation.reshape(-1, 9), new_offset], axis=1))


MESH = pl.DeviceIdType.MESH


def greet(peers):
    barrier = pltpu.get_barrier_semaphore()
    for peer in peers:
        pl.semaphore_signal(barrier, inc=1, device_id=peer, device_id_type=MESH)
    pl.semaphore_wait(barrier, len(peers))


def key_tile_kernel(n_pb, n_ka, x_ref, o_ref, send, recv, own):
    row, col = lax.axis_index("pb"), lax.axis_index("ka")
    per = n_pb // n_ka
    peers = [{"pb": lax.rem(row + d, n_pb)} for d in range(1, n_pb)]
    greet(peers)
    for slot in range(per):

        @pl.when(row == col * per + slot)
        def _():
            local = pltpu.make_async_copy(x_ref, o_ref.at[slot], own)
            local.start()
            copies = [
                pltpu.make_async_remote_copy(
                    src_ref=x_ref,
                    dst_ref=o_ref.at[slot],
                    send_sem=send.at[d],
                    recv_sem=recv.at[slot],
                    device_id=peer,
                    device_id_type=MESH,
                )
                for d, peer in enumerate(peers)
            ]
            for copy in copies:
                copy.start()
            for copy in copies:
                copy.wait_send()
            local.wait()

    for slot in range(per):

        @pl.when(row != col * per + slot)
        def _():
            pltpu.make_async_remote_copy(
                src_ref=x_ref,
                dst_ref=o_ref.at[slot],
                send_sem=send.at[0],
                recv_sem=recv.at[slot],
                device_id=peers[0],
                device_id_type=MESH,
            ).wait_recv()


def key_tile(packed, n_pb, n_ka):
    per = n_pb // n_ka
    return pl.pallas_call(
        functools.partial(key_tile_kernel, n_pb, n_ka),
        out_shape=jax.ShapeDtypeStruct((per,) + packed.shape, packed.dtype),
        in_specs=[pl.BlockSpec(memory_space=pltpu.VMEM)],
        out_specs=pl.BlockSpec(memory_space=pltpu.VMEM),
        scratch_shapes=[
            pltpu.SemaphoreType.DMA((n_pb - 1,)),
            pltpu.SemaphoreType.DMA((per,)),
            pltpu.SemaphoreType.DMA,
        ],
        compiler_params=pltpu.CompilerParams(collective_id=0, has_side_effects=True),
    )(packed)


def exchange_kernel(n_ka, sums_ref, stats_ref, sums_out, stats_out, send, recv, own):
    me = lax.axis_index("ka")
    peers = [lax.rem(me + d, n_ka) for d in range(1, n_ka)]
    greet([{"ka": peer} for peer in peers])
    copies = []
    for d, peer in enumerate(peers):
        for part, (source, target) in enumerate(((sums_ref, sums_out), (stats_ref, stats_out))):
            copy = pltpu.make_async_remote_copy(
                src_ref=source.at[peer],
                dst_ref=target.at[me],
                send_sem=send.at[2 * d + part],
                recv_sem=recv.at[2 * d + part],
                device_id={"ka": peer},
                device_id_type=MESH,
            )
            copy.start()
            copies.append(copy)
    for part, (source, target) in enumerate(((sums_ref, sums_out), (stats_ref, stats_out))):
        copy = pltpu.make_async_copy(source.at[me], target.at[me], own.at[part])
        copy.start()
        copies.append(copy)
    for copy in copies:
        copy.wait()


def exchange(sums, stats, n_ka):
    return pl.pallas_call(
        functools.partial(exchange_kernel, n_ka),
        out_shape=(
            jax.ShapeDtypeStruct(sums.shape, sums.dtype),
            jax.ShapeDtypeStruct(stats.shape, stats.dtype),
        ),
        in_specs=[pl.BlockSpec(memory_space=pltpu.VMEM)] * 2,
        out_specs=(pl.BlockSpec(memory_space=pltpu.VMEM),) * 2,
        scratch_shapes=[
            pltpu.SemaphoreType.DMA((2 * n_ka - 2,)),
            pltpu.SemaphoreType.DMA((2 * n_ka - 2,)),
            pltpu.SemaphoreType.DMA((2,)),
        ],
        compiler_params=pltpu.CompilerParams(collective_id=1, has_side_effects=True),
    )(sums, stats)


def gather_kernel(n_pb, n_ka, x_ref, o_ref, send, recv, own):
    row, col = lax.axis_index("pb"), lax.axis_index("ka")
    along_pb = [{"pb": lax.rem(row + d, n_pb)} for d in range(1, n_pb)]
    along_ka = [{"ka": lax.rem(col + d, n_ka)} for d in range(1, n_ka)]
    greet(along_pb + along_ka)
    copies = [pltpu.make_async_copy(x_ref, o_ref.at[col, row], own)] + [
        pltpu.make_async_remote_copy(
            src_ref=x_ref,
            dst_ref=o_ref.at[col, row],
            send_sem=send.at[d],
            recv_sem=recv.at[d],
            device_id=peer,
            device_id_type=MESH,
        )
        for d, peer in enumerate(along_pb)
    ]
    for copy in copies:
        copy.start()
    for copy in copies:
        copy.wait()
    copies = [
        pltpu.make_async_remote_copy(
            src_ref=o_ref.at[col],
            dst_ref=o_ref.at[col],
            send_sem=send.at[n_pb - 1 + d],
            recv_sem=recv.at[n_pb - 1 + d],
            device_id=peer,
            device_id_type=MESH,
        )
        for d, peer in enumerate(along_ka)
    ]
    for copy in copies:
        copy.start()
    for copy in copies:
        copy.wait()


def gather_rows(x, n_pb, n_ka):
    out = pl.pallas_call(
        functools.partial(gather_kernel, n_pb, n_ka),
        out_shape=jax.ShapeDtypeStruct((n_ka, n_pb) + x.shape, x.dtype),
        in_specs=[pl.BlockSpec(memory_space=pltpu.VMEM)],
        out_specs=pl.BlockSpec(memory_space=pltpu.VMEM),
        scratch_shapes=[
            pltpu.SemaphoreType.DMA((n_pb + n_ka - 2,)),
            pltpu.SemaphoreType.DMA((n_pb + n_ka - 2,)),
            pltpu.SemaphoreType.DMA,
        ],
        compiler_params=pltpu.CompilerParams(collective_id=2, has_side_effects=True),
    )(x)
    return jnp.transpose(out, (1, 0, 2, 3)).reshape(-1, x.shape[-1])


def edge_kernel(
    pair_ref, row_ref, key_ref, live_row, live_key, first, second, third, bias, scale, o_ref
):
    rows, keys, width = pair_ref.shape
    pair = pair_ref[...].reshape(rows * keys, width)
    hidden = jnp.dot(pair, first[...], preferred_element_type=jnp.float32)
    hidden = hidden.reshape(rows, keys, -1) + row_ref[...][:, None, :] + key_ref[...][None]
    hidden = jnp.maximum(hidden, 0.0).astype(jnp.bfloat16).reshape(rows * keys, -1)
    middle = jnp.dot(hidden, second[...], preferred_element_type=jnp.float32) + bias[...]
    middle = jnp.maximum(middle, 0.0).astype(jnp.bfloat16)
    result = pair.astype(jnp.float32) + jnp.dot(
        middle, third[...], preferred_element_type=jnp.float32
    )
    normed = layer_norm(result, scale[...]).reshape(rows, keys, width)
    live = live_row[...][:, None, :] * live_key[...][None]
    o_ref[...] = (normed * live).astype(o_ref.dtype)


def edge_transition(pair_rep, row_part, key_part, mask_rows, mask_keys, mats, bias, scale):
    rows, keys, width = pair_rep.shape
    step = 8
    live_row = jnp.broadcast_to(mask_rows.astype(jnp.float32)[:, None], (rows, width))
    live_key = jnp.broadcast_to(mask_keys.astype(jnp.float32)[:, None], (keys, width))

    def whole(array):
        return pl.BlockSpec(array.shape, lambda i: (0, 0))

    flat = [live_key, *mats, bias[None], scale[None]]
    return pl.pallas_call(
        edge_kernel,
        grid=(rows // step,),
        out_shape=jax.ShapeDtypeStruct(pair_rep.shape, jnp.bfloat16),
        in_specs=[
            pl.BlockSpec((step, keys, width), lambda i: (i, 0, 0)),
            pl.BlockSpec((step, row_part.shape[1]), lambda i: (i, 0)),
            whole(key_part),
            pl.BlockSpec((step, width), lambda i: (i, 0)),
        ]
        + [whole(array) for array in flat],
        out_specs=pl.BlockSpec((step, keys, width), lambda i: (i, 0, 0)),
    )(pair_rep, row_part, key_part, live_row, *flat)


def finish_rows(merged, rotation, offset, states, output_weight, attention_scales):
    features = ipa_features(merged, rotation, offset).astype(jnp.bfloat16)
    return layer_norm(
        states + jnp.dot(features, output_weight, preferred_element_type=jnp.float32),
        attention_scales,
    )


def on_device(
    node_states,
    frames,
    edge_states,
    chain_number,
    residue_index,
    padding_mask,
    query_weight,
    key_weight,
    value_weight,
    point_query,
    point_key,
    point_value,
    bias_weight,
    point_gamma,
    relpos_table,
    output_weight,
    attention_scales,
    layer_project,
    layer_output,
    layer_expand,
    layer_shrink,
    layer_scales,
    frame_weight,
    node_to_edge,
    edge_first,
    edge_second,
    edge_third,
    edge_biases,
    edge_scales,
):
    row_count = node_states.shape[0]
    key_count = edge_states.shape[1]
    row_first = lax.axis_index("pb") * row_count
    key_first = lax.axis_index("ka") * key_count
    n_pb, n_ka = lax.axis_size("pb"), lax.axis_size("ka")
    packed = jnp.concatenate([node_states, jnp.transpose(frames)], axis=1).astype(jnp.bfloat16)
    packed = jnp.pad(packed, ((0, 0), (0, -packed.shape[1] % 128)))
    tile = key_tile(packed, n_pb, n_ka).reshape(key_count, -1)
    key_input = tile[:, :C_S]
    key_rotation = tile[:, C_S : C_S + 9].astype(jnp.float32)
    key_offset = tile[:, C_S + 9 : C_S + 12].astype(jnp.float32)
    chain_rows = lax.dynamic_slice_in_dim(chain_number, row_first, row_count, 0)
    chain_keys = lax.dynamic_slice_in_dim(chain_number, key_first, key_count, 0)
    index_rows = lax.dynamic_slice_in_dim(residue_index, row_first, row_count, 0)
    index_keys = lax.dynamic_slice_in_dim(residue_index, key_first, key_count, 0)
    mask_rows = lax.dynamic_slice_in_dim(padding_mask, row_first, row_count, 0)
    mask_keys = lax.dynamic_slice_in_dim(padding_mask, key_first, key_count, 0)
    rotation, offset = jnp.transpose(frames[:9]), jnp.transpose(frames[9:12])
    row_input = node_states.astype(jnp.bfloat16)
    queries = head_split(
        jnp.dot(row_input, query_weight, preferred_element_type=jnp.float32).astype(jnp.bfloat16),
        HD,
    )
    key_vectors = head_split(
        jnp.dot(key_input, key_weight, preferred_element_type=jnp.float32).astype(jnp.bfloat16), HD
    )
    value_vectors = head_split(
        jnp.dot(key_input, value_weight, preferred_element_type=jnp.float32).astype(jnp.bfloat16),
        HD,
    )
    query_places = place_points(row_input, point_query, rotation, offset, QKP)
    key_places = place_points(key_input, point_key, key_rotation, key_offset, QKP)
    value_places = place_points(key_input, point_value, key_rotation, key_offset, VP)
    bins = relative_bins(chain_rows, index_rows, chain_keys, index_keys)
    onehot = (bins[:, :, None] == jnp.arange(RELBINS, dtype=jnp.int32)).astype(jnp.bfloat16)
    onehot = onehot.reshape(-1, RELBINS)
    table_top = lax.reduce_precision(relpos_table, 8, 7)
    table_high = table_top.astype(jnp.bfloat16)
    table_low = (relpos_table - table_top).astype(jnp.bfloat16)
    relative = (
        jnp.dot(onehot, table_high, preferred_element_type=jnp.float32)
        + jnp.dot(onehot, table_low, preferred_element_type=jnp.float32)
    ).reshape(row_count, key_count, -1)
    pair_rep = (edge_states.astype(jnp.float32) + relative).astype(jnp.bfloat16)
    logits = point_logits(
        queries, key_vectors, query_places, key_places, pair_rep, bias_weight, point_gamma
    )
    key_valid = (mask_keys == 1)[None, None, :]
    masked = jnp.where(key_valid, logits, NEG_FILL)
    local_top = jnp.max(masked, axis=-1)
    weights = jnp.where(key_valid, jnp.exp(masked - local_top[..., None]), 0.0)
    local_total = jnp.sum(weights, axis=-1)
    rounded = weights.astype(jnp.bfloat16)
    scalar_acc = jnp.einsum(
        "hij,jhd->ihd", rounded, value_vectors, preferred_element_type=jnp.float32
    )
    pair_acc = jnp.einsum("hij,ijc->ihc", rounded, pair_rep, preferred_element_type=jnp.float32)
    point_all = jnp.dot(
        weights.reshape(-1, key_count), value_places, precision=HIGHEST
    ).reshape(HEADS, row_count, -1)
    point_acc = jnp.sum(point_all * head_lanes(VP)[:, None, :], axis=0)
    part = row_count // n_ka
    sums = jnp.concatenate(
        [
            scalar_acc.reshape(row_count, -1),
            pair_acc.reshape(row_count, -1),
            point_acc[:, : HEADS * 3 * VP],
        ],
        axis=1,
    ).astype(jnp.bfloat16)
    used = sums.shape[1]
    sums = jnp.pad(sums, ((0, 0), (0, -used % 128))).reshape(n_ka, part, -1)
    stats = jnp.concatenate([jnp.transpose(local_top), jnp.transpose(local_total)], axis=1)
    stats = jnp.pad(stats, ((0, 0), (0, -stats.shape[1] % 128))).reshape(n_ka, part, -1)
    sums, stats = exchange(sums, stats, n_ka)
    tops, totals = stats[..., :HEADS], stats[..., HEADS : 2 * HEADS]
    factor = jnp.exp(tops - jnp.max(tops, axis=0))
    factor = factor / jnp.sum(totals * factor, axis=0)
    channels = pair_rep.shape[-1]
    spread = jnp.concatenate(
        [
            jnp.repeat(factor, HD, axis=2),
            jnp.repeat(factor, channels, axis=2),
            jnp.repeat(factor, 3 * VP, axis=2),
        ],
        axis=2,
    )
    merged = jnp.sum(sums[..., :used].astype(jnp.float32) * spread, axis=0)
    part_first = lax.axis_index("ka") * part
    first_states = finish_rows(
        merged,
        lax.dynamic_slice_in_dim(rotation, part_first, part, 0),
        lax.dynamic_slice_in_dim(offset, part_first, part, 0),
        lax.dynamic_slice_in_dim(node_states, part_first, part, 0),
        output_weight,
        attention_scales,
    )
    every_valid = padding_mask == 1
    whole_states = gather_rows(first_states.astype(jnp.bfloat16), n_pb, n_ka).astype(
        first_states.dtype
    )
    for layer_number in range(LAYERS):
        projection = layer_project[layer_number]
        key_value = jnp.dot(
            whole_states.astype(jnp.bfloat16),
            projection[:, C_S:],
            preferred_element_type=jnp.float32,
        ).astype(jnp.bfloat16)
        if layer_number == LAYERS - 1:
            whole_states = jnp.concatenate(
                [
                    lax.dynamic_slice_in_dim(whole_states, row_first, row_count, 0),
                    lax.dynamic_slice_in_dim(whole_states, key_first, key_count, 0),
                ],
                axis=0,
            )
        query_half = jnp.dot(
            whole_states.astype(jnp.bfloat16),
            projection[:, :C_S],
            preferred_element_type=jnp.float32,
        ).astype(jnp.bfloat16)
        whole_states = encoder_core(
            whole_states,
            query_half,
            key_value,
            every_valid,
            layer_output[layer_number],
            layer_expand[layer_number],
            layer_shrink[layer_number],
            layer_scales[layer_number],
        )
    second_states = whole_states[:row_count]
    key_second = whole_states[row_count:]
    frames_out = update_frames(second_states, frames, frame_weight)
    row_project = jnp.dot(
        second_states.astype(jnp.bfloat16), node_to_edge[:, :EH], preferred_element_type=jnp.float32
    )
    key_project = jnp.dot(
        key_second.astype(jnp.bfloat16), node_to_edge[:, EH:], preferred_element_type=jnp.float32
    )
    edges_out = edge_transition(
        pair_rep,
        row_project,
        key_project + edge_biases[0],
        mask_rows,
        mask_keys,
        (edge_first, edge_second, edge_third),
        edge_biases[1],
        edge_scales,
    )
    return (second_states, frames_out, edges_out)


def solution(mesh):
    placed = (
        P("pb", None),
        P(None, "pb"),
        P("pb", "ka", None),
        P(),
        P(),
        P(),
        P(),
        P(),
        P(),
        P(),
        P(),
        P(),
        P(),
        P(),
        P(),
        P(),
        P(),
        P(),
        P(),
        P(),
        P(),
        P(),
        P(),
        P(),
        P(),
        P(),
        P(),
        P(),
        P(),
    )
    return jax.shard_map(
        on_device,
        mesh=mesh,
        in_specs=placed,
        out_specs=(P("pb", None), P(None, "pb"), P("pb", "ka", None)),
        check_vma=False,
    )
```

```python
import functools
import math

import jax
import jax.numpy as jnp
import numpy as np
from jax import lax
from jax.experimental import pallas as pl
from jax.experimental.pallas import tpu as pltpu
from jax.sharding import PartitionSpec as P

C_S = 256
HEADS = 8
HD = 256
QKP = 8
VP = 12
EH = 384
RELBINS = 128
LAYERS = 2
TF_HD = 64


HIGHEST = lax.Precision.HIGHEST
NEG_FILL = -1000000000.0


def layer_norm(values, scales):
    centered = values - jnp.mean(values, axis=-1, keepdims=True)
    variance = jnp.mean(centered * centered, axis=-1, keepdims=True)
    return centered * lax.rsqrt(variance + 1e-05) * scales


def frame_parts(frames):
    rotation = jnp.transpose(frames[:9]).reshape(-1, 3, 3)
    offset = jnp.transpose(frames[9:12])
    return (rotation, offset)


def head_split(matrix, width):
    return matrix.reshape(matrix.shape[0], -1, width)


def lane_parts(count):
    width = HEADS * 3 * count
    padded = -(-width // 128) * 128
    lane = np.arange(padded)
    real = lane < width
    head, comp, point = lane // (3 * count), lane // count % 3, lane % count
    return padded, real, head, comp, point


def pick(sources, size, dtype):
    sources = jnp.asarray(sources, jnp.int32)
    return (jnp.arange(size, dtype=jnp.int32)[:, None] == sources[None, :]).astype(dtype)


def component_copies(count, size, dtype):
    padded, real, head, comp, point = lane_parts(count)
    copies = [np.where(real, (head * 3 + d) * count + point, -1) for d in range(3)]
    return pick(np.concatenate(copies), size, dtype)


def rotation_lanes(rotation, count, inverse):
    padded, real, head, comp, point = lane_parts(count)
    entries = [np.where(real, d * 3 + comp if inverse else comp * 3 + d, -1) for d in range(3)]
    return jnp.dot(
        rotation, pick(np.concatenate(entries), 9, jnp.float32), precision=HIGHEST
    )


def offset_lanes(offset, count):
    padded, real, head, comp, point = lane_parts(count)
    return jnp.dot(offset, pick(np.where(real, comp, -1), 3, jnp.float32), precision=HIGHEST)


def head_lanes(count):
    padded, real, head, comp, point = lane_parts(count)
    return pick(np.where(real, head, -1), HEADS, jnp.float32)


def add_thirds(values):
    third = values.shape[1] // 3
    return values[:, :third] + values[:, third : 2 * third] + values[:, 2 * third :]


def place_points(features, weight, rotation, offset, count):
    copies = component_copies(count, weight.shape[1], weight.dtype)
    spread = jnp.dot(weight, copies, preferred_element_type=jnp.float32).astype(weight.dtype)
    local = jnp.dot(features, spread, preferred_element_type=jnp.float32)
    return add_thirds(local * rotation_lanes(rotation, count, False)) + offset_lanes(offset, count)


def relative_bins(chain_rows, index_rows, chain_cols, index_cols):
    reach = (RELBINS - 2) // 2
    gap_class = jnp.clip(index_rows[:, None] - index_cols[None, :], -reach, reach) + reach
    same_chain = chain_rows[:, None] == chain_cols[None, :]
    return jnp.where(same_chain, gap_class, RELBINS - 1)


def point_logits(
    queries, key_vectors, query_places, key_places, pair_rep, bias_weight, point_gamma
):
    scalar = jnp.einsum(
        "ihd,jhd->hij", queries, key_vectors, preferred_element_type=jnp.float32
    ) / math.sqrt(HD)
    pair_bias = jnp.einsum("ijc,ch->hij", pair_rep, bias_weight, preferred_element_type=jnp.float32)
    heads = head_lanes(QKP)
    query_square = lax.dot_general(
        heads, query_places * query_places, (((1,), (1,)), ((), ())), precision=HIGHEST
    )
    key_square = lax.dot_general(
        heads, key_places * key_places, (((1,), (1,)), ((), ())), precision=HIGHEST
    )
    by_head = (query_places[None] * heads[:, None, :]).reshape(-1, query_places.shape[1])
    cross = lax.dot_general(
        by_head, key_places, (((1,), (1,)), ((), ())), precision=HIGHEST
    ).reshape(HEADS, query_places.shape[0], -1)
    distance = query_square[:, :, None] + key_square[:, None, :] - 2.0 * cross
    weight_points = math.sqrt(2.0 / (9.0 * QKP))
    return math.sqrt(1.0 / 3.0) * (
        scalar + pair_bias - 0.5 * weight_points * point_gamma[:, None, None] * distance
    )


def ipa_features(merged, rotation, offset):
    points_first = merged.shape[1] - HEADS * 3 * VP
    padded, real, head, comp, point = lane_parts(VP)
    point_global = jnp.pad(
        merged[:, points_first:], ((0, 0), (0, padded - HEADS * 3 * VP))
    )
    moved = point_global - offset_lanes(offset, VP)
    rotated = jnp.dot(
        moved, component_copies(VP, padded, jnp.float32), precision=HIGHEST
    ) * rotation_lanes(rotation, VP, True)
    local = add_thirds(rotated)
    owner = np.where(real, head * VP + point, -1)
    same = jnp.transpose(pick(owner, HEADS * VP, jnp.float32))
    lengths = jnp.sqrt(jnp.dot(local * local, same, precision=HIGHEST) + 1e-08)
    return jnp.concatenate(
        [merged[:, :points_first], local[:, : HEADS * 3 * VP], lengths], axis=1
    )


def encoder_rows(states, key_value, fill, project, output, expand, shrink, scales):
    queries = jnp.dot(
        states.astype(jnp.bfloat16), project[:, :C_S], preferred_element_type=jnp.float32
    ).astype(jnp.bfloat16) * jnp.asarray(1.0 / math.sqrt(TF_HD), jnp.bfloat16)
    owner = lax.broadcasted_iota(jnp.int32, (1, C_S), 1) // TF_HD
    context = jnp.zeros(states.shape, jnp.float32)
    for head in range(C_S // TF_HD):
        mine = owner == head
        only = jnp.where(mine, 1.0, 0.0)
        scores = lax.dot_general(
            queries * only.astype(jnp.bfloat16),
            key_value[:, :C_S],
            (((1,), (1,)), ((), ())),
            preferred_element_type=jnp.float32,
        )
        scores = scores + fill
        weights = jnp.exp(scores - jnp.max(scores, axis=-1, keepdims=True))
        inverse = 1.0 / jnp.sum(weights, axis=-1, keepdims=True)
        mixed = jnp.dot(
            weights.astype(jnp.bfloat16),
            key_value[:, C_S:],
            preferred_element_type=jnp.float32,
        )
        context = context + mixed * (inverse * only)
    middle = layer_norm(
        states
        + jnp.dot(context.astype(jnp.bfloat16), output, preferred_element_type=jnp.float32),
        scales[0:1],
    )
    hidden = jnp.maximum(
        jnp.dot(middle.astype(jnp.bfloat16), expand, preferred_element_type=jnp.float32), 0.0
    ).astype(jnp.bfloat16)
    return layer_norm(
        middle + jnp.dot(hidden, shrink, preferred_element_type=jnp.float32), scales[1:2]
    )


def encoder_kernel(
    states_ref,
    fill_ref,
    project,
    output,
    expand,
    shrink,
    scales,
    to_edge,
    bias,
    second_ref,
    row_ref,
    key_ref,
    old,
    new,
    key_value,
):
    count = states_ref.shape[0]
    rows, keys = row_ref.shape[0], key_ref.shape[0]
    chunk = math.gcd(count, 128)

    def apply(states, layer):
        return encoder_rows(
            states,
            key_value[...],
            fill_ref[...],
            project[layer],
            output[layer],
            expand[layer],
            shrink[layer],
            scales[layer],
        )

    old[...] = states_ref[...].astype(jnp.float32)
    buffers = (old, new)
    for layer in range(LAYERS):
        source, target = buffers[layer % 2], buffers[(layer + 1) % 2]
        key_value[...] = jnp.dot(
            source[...].astype(jnp.bfloat16),
            project[layer][:, C_S:],
            preferred_element_type=jnp.float32,
        ).astype(jnp.bfloat16)
        if layer < LAYERS - 1:

            def step(index, carry):
                window = pl.ds(pl.multiple_of(index * chunk, chunk), chunk)
                target[window, :] = apply(source[window, :], layer)
                return carry

            lax.fori_loop(0, count // chunk, step, 0)
        else:
            row_first = pl.multiple_of(lax.axis_index("pb") * rows, rows)
            key_first = pl.multiple_of(lax.axis_index("ka") * keys, keys)
            second = apply(source[pl.ds(row_first, rows), :], layer)
            second_ref[...] = second
            row_ref[...] = jnp.dot(
                second.astype(jnp.bfloat16), to_edge[:, :EH], preferred_element_type=jnp.float32
            )
            final = apply(source[pl.ds(key_first, keys), :], layer)
            key_ref[...] = (
                jnp.dot(
                    final.astype(jnp.bfloat16), to_edge[:, EH:], preferred_element_type=jnp.float32
                )
                + bias[...]
            )


def encode(states, valid, rows, keys, project, output, expand, shrink, scales, to_edge, bias):
    fill = jnp.where(valid, 0.0, NEG_FILL)[None]
    count = states.shape[0]
    return pl.pallas_call(
        encoder_kernel,
        out_shape=(
            jax.ShapeDtypeStruct((rows, C_S), jnp.float32),
            jax.ShapeDtypeStruct((rows, EH), jnp.float32),
            jax.ShapeDtypeStruct((keys, EH), jnp.float32),
        ),
        in_specs=[pl.BlockSpec(memory_space=pltpu.VMEM)] * 9,
        out_specs=(pl.BlockSpec(memory_space=pltpu.VMEM),) * 3,
        scratch_shapes=[
            pltpu.VMEM((count, C_S), jnp.float32),
            pltpu.VMEM((count, C_S), jnp.float32),
            pltpu.VMEM((count, 2 * C_S), jnp.bfloat16),
        ],
    )(states, fill, project, output, expand, shrink, scales, to_edge, bias[None])


def update_frames(states, frames, frame_weight):
    update = jnp.dot(states, frame_weight, precision=HIGHEST)
    length = jnp.sqrt(
        1.0
        + update[:, 0] * update[:, 0]
        + update[:, 1] * update[:, 1]
        + update[:, 2] * update[:, 2]
    )
    real_part = 1.0 / length
    first_imag = update[:, 0] / length
    second_imag = update[:, 1] / length
    third_imag = update[:, 2] / length
    row_one = jnp.stack(
        [
            real_part * real_part
            + first_imag * first_imag
            - second_imag * second_imag
            - third_imag * third_imag,
            2.0 * (first_imag * second_imag - real_part * third_imag),
            2.0 * (first_imag * third_imag + real_part * second_imag),
        ],
        axis=1,
    )
    row_two = jnp.stack(
        [
            2.0 * (first_imag * second_imag + real_part * third_imag),
            real_part * real_part
            - first_imag * first_imag
            + second_imag * second_imag
            - third_imag * third_imag,
            2.0 * (second_imag * third_imag - real_part * first_imag),
        ],
        axis=1,
    )
    row_three = jnp.stack(
        [
            2.0 * (first_imag * third_imag - real_part * second_imag),
            2.0 * (second_imag * third_imag + real_part * first_imag),
            real_part * real_part
            - first_imag * first_imag
            - second_imag * second_imag
            + third_imag * third_imag,
        ],
        axis=1,
    )
    turn = jnp.stack([row_one, row_two, row_three], axis=1)
    rotation, offset = frame_parts(frames)
    new_rotation = jnp.einsum("rcd,rde->rce", rotation, turn, precision=HIGHEST)
    new_offset = jnp.einsum("rcd,rd->rc", rotation, update[:, 3:6], precision=HIGHEST) + offset
    return jnp.transpose(jnp.concatenate([new_rotation.reshape(-1, 9), new_offset], axis=1))


MESH = pl.DeviceIdType.MESH


def greet(peers):
    barrier = pltpu.get_barrier_semaphore()
    for peer in peers:
        pl.semaphore_signal(barrier, inc=1, device_id=peer, device_id_type=MESH)
    pl.semaphore_wait(barrier, len(peers))


def key_tile_kernel(n_pb, n_ka, x_ref, o_ref, send, recv, own):
    row, col = lax.axis_index("pb"), lax.axis_index("ka")
    per = n_pb // n_ka
    peers = [{"pb": lax.rem(row + d, n_pb)} for d in range(1, n_pb)]
    greet(peers)
    for slot in range(per):

        @pl.when(row == col * per + slot)
        def _():
            local = pltpu.make_async_copy(x_ref, o_ref.at[slot], own)
            local.start()
            copies = [
                pltpu.make_async_remote_copy(
                    src_ref=x_ref,
                    dst_ref=o_ref.at[slot],
                    send_sem=send.at[d],
                    recv_sem=recv.at[slot],
                    device_id=peer,
                    device_id_type=MESH,
                )
                for d, peer in enumerate(peers)
            ]
            for copy in copies:
                copy.start()
            for copy in copies:
                copy.wait_send()
            local.wait()

    for slot in range(per):

        @pl.when(row != col * per + slot)
        def _():
            pltpu.make_async_remote_copy(
                src_ref=x_ref,
                dst_ref=o_ref.at[slot],
                send_sem=send.at[0],
                recv_sem=recv.at[slot],
                device_id=peers[0],
                device_id_type=MESH,
            ).wait_recv()


def key_tile(packed, n_pb, n_ka):
    per = n_pb // n_ka
    return pl.pallas_call(
        functools.partial(key_tile_kernel, n_pb, n_ka),
        out_shape=jax.ShapeDtypeStruct((per,) + packed.shape, packed.dtype),
        in_specs=[pl.BlockSpec(memory_space=pltpu.VMEM)],
        out_specs=pl.BlockSpec(memory_space=pltpu.VMEM),
        scratch_shapes=[
            pltpu.SemaphoreType.DMA((n_pb - 1,)),
            pltpu.SemaphoreType.DMA((per,)),
            pltpu.SemaphoreType.DMA,
        ],
        compiler_params=pltpu.CompilerParams(collective_id=0, has_side_effects=True),
    )(packed)


def exchange_kernel(n_ka, sums_ref, stats_ref, sums_out, stats_out, send, recv, own):
    me = lax.axis_index("ka")
    peers = [lax.rem(me + d, n_ka) for d in range(1, n_ka)]
    greet([{"ka": peer} for peer in peers])
    copies = []
    for d, peer in enumerate(peers):
        for part, (source, target) in enumerate(((sums_ref, sums_out), (stats_ref, stats_out))):
            copy = pltpu.make_async_remote_copy(
                src_ref=source.at[peer],
                dst_ref=target.at[me],
                send_sem=send.at[2 * d + part],
                recv_sem=recv.at[2 * d + part],
                device_id={"ka": peer},
                device_id_type=MESH,
            )
            copy.start()
            copies.append(copy)
    for part, (source, target) in enumerate(((sums_ref, sums_out), (stats_ref, stats_out))):
        copy = pltpu.make_async_copy(source.at[me], target.at[me], own.at[part])
        copy.start()
        copies.append(copy)
    for copy in copies:
        copy.wait()


def exchange(sums, stats, n_ka):
    return pl.pallas_call(
        functools.partial(exchange_kernel, n_ka),
        out_shape=(
            jax.ShapeDtypeStruct(sums.shape, sums.dtype),
            jax.ShapeDtypeStruct(stats.shape, stats.dtype),
        ),
        in_specs=[pl.BlockSpec(memory_space=pltpu.VMEM)] * 2,
        out_specs=(pl.BlockSpec(memory_space=pltpu.VMEM),) * 2,
        scratch_shapes=[
            pltpu.SemaphoreType.DMA((2 * n_ka - 2,)),
            pltpu.SemaphoreType.DMA((2 * n_ka - 2,)),
            pltpu.SemaphoreType.DMA((2,)),
        ],
        compiler_params=pltpu.CompilerParams(collective_id=1, has_side_effects=True),
    )(sums, stats)


def gather_kernel(n_pb, n_ka, x_ref, o_ref, send, recv, own):
    row, col = lax.axis_index("pb"), lax.axis_index("ka")
    along_pb = [{"pb": lax.rem(row + d, n_pb)} for d in range(1, n_pb)]
    along_ka = [{"ka": lax.rem(col + d, n_ka)} for d in range(1, n_ka)]
    greet(along_pb + along_ka)
    copies = [pltpu.make_async_copy(x_ref, o_ref.at[col, row], own)] + [
        pltpu.make_async_remote_copy(
            src_ref=x_ref,
            dst_ref=o_ref.at[col, row],
            send_sem=send.at[d],
            recv_sem=recv.at[d],
            device_id=peer,
            device_id_type=MESH,
        )
        for d, peer in enumerate(along_pb)
    ]
    for copy in copies:
        copy.start()
    for copy in copies:
        copy.wait()
    copies = [
        pltpu.make_async_remote_copy(
            src_ref=o_ref.at[col],
            dst_ref=o_ref.at[col],
            send_sem=send.at[n_pb - 1 + d],
            recv_sem=recv.at[n_pb - 1 + d],
            device_id=peer,
            device_id_type=MESH,
        )
        for d, peer in enumerate(along_ka)
    ]
    for copy in copies:
        copy.start()
    for copy in copies:
        copy.wait()


def gather_rows(x, n_pb, n_ka):
    out = pl.pallas_call(
        functools.partial(gather_kernel, n_pb, n_ka),
        out_shape=jax.ShapeDtypeStruct((n_ka, n_pb) + x.shape, x.dtype),
        in_specs=[pl.BlockSpec(memory_space=pltpu.VMEM)],
        out_specs=pl.BlockSpec(memory_space=pltpu.VMEM),
        scratch_shapes=[
            pltpu.SemaphoreType.DMA((n_pb + n_ka - 2,)),
            pltpu.SemaphoreType.DMA((n_pb + n_ka - 2,)),
            pltpu.SemaphoreType.DMA,
        ],
        compiler_params=pltpu.CompilerParams(collective_id=2, has_side_effects=True),
    )(x)
    return jnp.transpose(out, (1, 0, 2, 3)).reshape(-1, x.shape[-1])


def edge_kernel(
    pair_ref, row_ref, key_ref, live_row, live_key, first, second, third, bias, scale, o_ref
):
    rows, keys, width = pair_ref.shape
    pair = pair_ref[...].reshape(rows * keys, width)
    hidden = jnp.dot(pair, first[...], preferred_element_type=jnp.float32)
    hidden = hidden.reshape(rows, keys, -1) + row_ref[...][:, None, :] + key_ref[...][None]
    hidden = jnp.maximum(hidden, 0.0).astype(jnp.bfloat16).reshape(rows * keys, -1)
    middle = jnp.dot(hidden, second[...], preferred_element_type=jnp.float32) + bias[...]
    middle = jnp.maximum(middle, 0.0).astype(jnp.bfloat16)
    result = pair.astype(jnp.float32) + jnp.dot(
        middle, third[...], preferred_element_type=jnp.float32
    )
    normed = layer_norm(result, scale[...]).reshape(rows, keys, width)
    live = live_row[...][:, None, :] * live_key[...][None]
    o_ref[...] = (normed * live).astype(o_ref.dtype)


def edge_transition(pair_rep, row_part, key_part, mask_rows, mask_keys, mats, bias, scale):
    rows, keys, width = pair_rep.shape
    step = 8
    live_row = jnp.broadcast_to(mask_rows.astype(jnp.float32)[:, None], (rows, width))
    live_key = jnp.broadcast_to(mask_keys.astype(jnp.float32)[:, None], (keys, width))

    def whole(array):
        return pl.BlockSpec(array.shape, lambda i: (0, 0))

    flat = [live_key, *mats, bias[None], scale[None]]
    return pl.pallas_call(
        edge_kernel,
        grid=(rows // step,),
        out_shape=jax.ShapeDtypeStruct(pair_rep.shape, jnp.bfloat16),
        in_specs=[
            pl.BlockSpec((step, keys, width), lambda i: (i, 0, 0)),
            pl.BlockSpec((step, row_part.shape[1]), lambda i: (i, 0)),
            whole(key_part),
            pl.BlockSpec((step, width), lambda i: (i, 0)),
        ]
        + [whole(array) for array in flat],
        out_specs=pl.BlockSpec((step, keys, width), lambda i: (i, 0, 0)),
    )(pair_rep, row_part, key_part, live_row, *flat)


def finish_rows(merged, rotation, offset, states, output_weight, attention_scales):
    features = ipa_features(merged, rotation, offset).astype(jnp.bfloat16)
    return layer_norm(
        states + jnp.dot(features, output_weight, preferred_element_type=jnp.float32),
        attention_scales,
    )


def on_device(
    node_states,
    frames,
    edge_states,
    chain_number,
    residue_index,
    padding_mask,
    query_weight,
    key_weight,
    value_weight,
    point_query,
    point_key,
    point_value,
    bias_weight,
    point_gamma,
    relpos_table,
    output_weight,
    attention_scales,
    layer_project,
    layer_output,
    layer_expand,
    layer_shrink,
    layer_scales,
    frame_weight,
    node_to_edge,
    edge_first,
    edge_second,
    edge_third,
    edge_biases,
    edge_scales,
):
    row_count = node_states.shape[0]
    key_count = edge_states.shape[1]
    row_first = lax.axis_index("pb") * row_count
    key_first = lax.axis_index("ka") * key_count
    n_pb, n_ka = lax.axis_size("pb"), lax.axis_size("ka")
    packed = jnp.concatenate([node_states, jnp.transpose(frames)], axis=1).astype(jnp.bfloat16)
    packed = jnp.pad(packed, ((0, 0), (0, -packed.shape[1] % 128)))
    tile = key_tile(packed, n_pb, n_ka).reshape(key_count, -1)
    key_input = tile[:, :C_S]
    key_rotation = tile[:, C_S : C_S + 9].astype(jnp.float32)
    key_offset = tile[:, C_S + 9 : C_S + 12].astype(jnp.float32)
    chain_rows = lax.dynamic_slice_in_dim(chain_number, row_first, row_count, 0)
    chain_keys = lax.dynamic_slice_in_dim(chain_number, key_first, key_count, 0)
    index_rows = lax.dynamic_slice_in_dim(residue_index, row_first, row_count, 0)
    index_keys = lax.dynamic_slice_in_dim(residue_index, key_first, key_count, 0)
    mask_rows = lax.dynamic_slice_in_dim(padding_mask, row_first, row_count, 0)
    mask_keys = lax.dynamic_slice_in_dim(padding_mask, key_first, key_count, 0)
    rotation, offset = jnp.transpose(frames[:9]), jnp.transpose(frames[9:12])
    row_input = node_states.astype(jnp.bfloat16)
    queries = head_split(
        jnp.dot(row_input, query_weight, preferred_element_type=jnp.float32).astype(jnp.bfloat16),
        HD,
    )
    key_vectors = head_split(
        jnp.dot(key_input, key_weight, preferred_element_type=jnp.float32).astype(jnp.bfloat16), HD
    )
    value_vectors = head_split(
        jnp.dot(key_input, value_weight, preferred_element_type=jnp.float32).astype(jnp.bfloat16),
        HD,
    )
    query_places = place_points(row_input, point_query, rotation, offset, QKP)
    key_places = place_points(key_input, point_key, key_rotation, key_offset, QKP)
    value_places = place_points(key_input, point_value, key_rotation, key_offset, VP)
    bins = relative_bins(chain_rows, index_rows, chain_keys, index_keys)
    onehot = (bins[:, :, None] == jnp.arange(RELBINS, dtype=jnp.int32)).astype(jnp.bfloat16)
    onehot = onehot.reshape(-1, RELBINS)
    table_top = lax.reduce_precision(relpos_table, 8, 7)
    table_high = table_top.astype(jnp.bfloat16)
    table_low = (relpos_table - table_top).astype(jnp.bfloat16)
    relative = (
        jnp.dot(onehot, table_high, preferred_element_type=jnp.float32)
        + jnp.dot(onehot, table_low, preferred_element_type=jnp.float32)
    ).reshape(row_count, key_count, -1)
    pair_rep = (edge_states.astype(jnp.float32) + relative).astype(jnp.bfloat16)
    logits = point_logits(
        queries, key_vectors, query_places, key_places, pair_rep, bias_weight, point_gamma
    )
    key_valid = (mask_keys == 1)[None, None, :]
    masked = jnp.where(key_valid, logits, NEG_FILL)
    local_top = jnp.max(masked, axis=-1)
    weights = jnp.where(key_valid, jnp.exp(masked - local_top[..., None]), 0.0)
    local_total = jnp.sum(weights, axis=-1)
    rounded = weights.astype(jnp.bfloat16)
    scalar_acc = jnp.einsum(
        "hij,jhd->ihd", rounded, value_vectors, preferred_element_type=jnp.float32
    )
    pair_acc = jnp.einsum("hij,ijc->ihc", rounded, pair_rep, preferred_element_type=jnp.float32)
    point_all = jnp.dot(
        weights.reshape(-1, key_count), value_places, precision=HIGHEST
    ).reshape(HEADS, row_count, -1)
    point_acc = jnp.sum(point_all * head_lanes(VP)[:, None, :], axis=0)
    part = row_count // n_ka
    sums = jnp.concatenate(
        [
            scalar_acc.reshape(row_count, -1),
            pair_acc.reshape(row_count, -1),
            point_acc[:, : HEADS * 3 * VP],
        ],
        axis=1,
    ).astype(jnp.bfloat16)
    used = sums.shape[1]
    sums = jnp.pad(sums, ((0, 0), (0, -used % 128))).reshape(n_ka, part, -1)
    stats = jnp.concatenate([jnp.transpose(local_top), jnp.transpose(local_total)], axis=1)
    stats = jnp.pad(stats, ((0, 0), (0, -stats.shape[1] % 128))).reshape(n_ka, part, -1)
    sums, stats = exchange(sums, stats, n_ka)
    tops, totals = stats[..., :HEADS], stats[..., HEADS : 2 * HEADS]
    factor = jnp.exp(tops - jnp.max(tops, axis=0))
    factor = factor / jnp.sum(totals * factor, axis=0)
    channels = pair_rep.shape[-1]
    spread = jnp.concatenate(
        [
            jnp.repeat(factor, HD, axis=2),
            jnp.repeat(factor, channels, axis=2),
            jnp.repeat(factor, 3 * VP, axis=2),
        ],
        axis=2,
    )
    merged = jnp.sum(sums[..., :used].astype(jnp.float32) * spread, axis=0)
    part_first = lax.axis_index("ka") * part
    first_states = finish_rows(
        merged,
        lax.dynamic_slice_in_dim(rotation, part_first, part, 0),
        lax.dynamic_slice_in_dim(offset, part_first, part, 0),
        lax.dynamic_slice_in_dim(node_states, part_first, part, 0),
        output_weight,
        attention_scales,
    )
    every_valid = padding_mask == 1
    whole_states = gather_rows(first_states.astype(jnp.bfloat16), n_pb, n_ka)
    second_states, row_project, key_project = encode(
        whole_states,
        every_valid,
        row_count,
        key_count,
        layer_project,
        layer_output,
        layer_expand,
        layer_shrink,
        layer_scales,
        node_to_edge,
        edge_biases[0],
    )
    frames_out = update_frames(second_states, frames, frame_weight)
    edges_out = edge_transition(
        pair_rep,
        row_project,
        key_project,
        mask_rows,
        mask_keys,
        (edge_first, edge_second, edge_third),
        edge_biases[1],
        edge_scales,
    )
    return (second_states, frames_out, edges_out)


def solution(mesh):
    placed = (
        P("pb", None),
        P(None, "pb"),
        P("pb", "ka", None),
        P(),
        P(),
        P(),
        P(),
        P(),
        P(),
        P(),
        P(),
        P(),
        P(),
        P(),
        P(),
        P(),
        P(),
        P(),
        P(),
        P(),
        P(),
        P(),
        P(),
        P(),
        P(),
        P(),
        P(),
        P(),
        P(),
    )
    return jax.shard_map(
        on_device,
        mesh=mesh,
        in_specs=placed,
        out_specs=(P("pb", None), P(None, "pb"), P("pb", "ka", None)),
        check_vma=False,
    )
```
